256 devices in a mesh: section: 16 (over x, z_hi, core), rows: 16 (over y, z_lo).
Axes of the slice: x: 4, y: 4, z: 8 (z_hi: 2, z_lo: 4; z = z_hi * 4 + z_lo), core: 2. Of those that a mesh axis runs over, the one named last changes fastest.
Arguments:
- fwd_in: bfloat16 [16, 256, 32, 512], P('section', 'rows'), may hold values from -6 to 6
- grad_in: bfloat16 [16, 256, 32, 512], P('section', 'rows'), may hold values from -6 to 6
- saved_in: bfloat16 [16, 256, 32, 512], P('section', 'rows'), may hold values from -6 to 6
- mirror_held: bfloat16 [16, 256, 32, 512], P('section', 'rows'), may hold values from -6 to 6
- target: bfloat16 [256, 32, 512], P('rows'), may hold values from -6 to 6
- w_first: bfloat16 [16, 3, 3, 512, 512], P('section'), may hold values from -0.09375 to 0.09375
- w_second: bfloat16 [16, 3, 3, 512, 512], P('section'), may hold values from -0.09375 to 0.09375
Outputs:
- fwd_next: bfloat16 [16, 256, 32, 512], P('section', 'rows')
- grad_next: bfloat16 [16, 256, 32, 512], P('section', 'rows')
- mirror_next: bfloat16 [16, 256, 32, 512], P('section', 'rows')
The draws below stay inside these ranges and needn't reach their ends.
All inputs are finite; a program needn't handle non-finite values.
Results may differ from the reference program's by a relative error of at most 0.0085.
Values may be sent and summed in bfloat16 or wider, within the bound.
No kernel may reach another device: no remote copies, remote signals or barrier semaphores. Data moves between devices by JAX's collectives and lax.ppermute only.
A program may use at most 64 MiB of HBM per device.

```python
import jax
import jax.numpy as jnp
from jax import lax

C = 512
W = 32
SECTIONS = 16
H = 256


def block_scale(own_key, shape, pieces, least, top_value):
    level, own = 1.0, jax.random.fold_in(own_key, 6)
    for dim, blocks in pieces:
        draws = jnp.exp(jax.random.uniform(jax.random.fold_in(own, dim), (blocks,), jnp.float32, least / len(pieces), top_value / len(pieces)))
        level = level * jnp.repeat(draws, shape[dim] // blocks).reshape([-1 if axis == dim else 1 for axis in range(len(shape))])
    return level


def noise(stream_key, extent, width, limit, pieces=(), kind=jnp.bfloat16):
    result = jax.random.normal(stream_key, extent, jnp.float32) * width
    if len(pieces) > 0:
        result = block_scale(stream_key, extent, pieces, -0.22, 0.18) * result
    return jnp.clip(result, min=-limit, max=limit).astype(kind)


def setup_inputs(seed: int = 0) -> dict:
    key_of = jax.random.split(jax.random.key(seed), 8)
    fwd_in = noise(key_of[0], (SECTIONS, H, W, C), 1.0, 6.0, ((0, 16), (1, 16)))
    grad_in = noise(key_of[1], (SECTIONS, H, W, C), 1.0, 6.0, ((0, 16), (1, 16)))
    saved_in = noise(key_of[2], (SECTIONS, H, W, C), 1.0, 6.0, ((0, 16), (1, 16)))
    mirror_held = noise(key_of[3], (SECTIONS, H, W, C), 1.0, 6.0, ((0, 16), (1, 16)))
    target = noise(key_of[4], (H, W, C), 1.0, 6.0, ((0, 16),))
    w_first = noise(key_of[5], (SECTIONS, 3, 3, C, C), (9 * C) ** -0.5, 0.09375, ((0, 16),))
    w_second = noise(key_of[6], (SECTIONS, 3, 3, C, C), (9 * C) ** -0.5, 0.09375, ((0, 16),))
    return dict(fwd_in=fwd_in, grad_in=grad_in, saved_in=saved_in, mirror_held=mirror_held, target=target, w_first=w_first, w_second=w_second)


def conv_same(field, kernel):
    return lax.conv_general_dilated(field[None], kernel, (1, 1), ((1, 1), (1, 1)), dimension_numbers=("NHWC", "HWIO", "NHWC"), preferred_element_type=jnp.float32)[0]


def flipped(kernel):
    return jnp.transpose(kernel[::-1, ::-1], (0, 1, 3, 2))


def silu_slope(pre):
    sig = jax.nn.sigmoid(pre)
    return sig * (1.0 + pre * (1.0 - sig))


def reference(fwd_in, grad_in, saved_in, mirror_held, target, w_first, w_second):
    sections = fwd_in.shape[0]

    def one_section(items):
        index, act, grad, saved, held, kern_one, kern_two = items
        decoder = (index >= sections // 2).astype(jnp.float32)
        is_last = index == sections - 1
        block_in = act.astype(jnp.float32) + decoder * held.astype(jnp.float32)
        block_b = block_in.astype(jnp.bfloat16)
        hidden = jax.nn.silu(conv_same(block_b, kern_one)).astype(jnp.bfloat16)
        output = (block_in + conv_same(hidden, kern_two)).astype(jnp.bfloat16)
        g_top = jnp.where(is_last, output.astype(jnp.float32) - target.astype(jnp.float32), grad.astype(jnp.float32) + (1.0 - decoder) * held.astype(jnp.float32)).astype(jnp.bfloat16)
        kept = jnp.where(is_last, block_b, saved)
        pre = conv_same(kept, kern_one)
        g_mid = (silu_slope(pre) * conv_same(g_top, flipped(kern_two))).astype(jnp.bfloat16)
        g_low = (g_top.astype(jnp.float32) + conv_same(g_mid, flipped(kern_one))).astype(jnp.bfloat16)
        return output, g_low

    indices = jnp.arange(sections, dtype=jnp.int32)
    outputs, lows = lax.map(one_section, (indices, fwd_in, grad_in, saved_in, mirror_held, w_first, w_second))
    zero = jnp.zeros_like(outputs[:1])
    fwd_next = jnp.concatenate([zero, outputs[:-1]], axis=0)
    grad_next = jnp.concatenate([lows[1:], zero], axis=0)
    decoder_mask = (indices >= sections // 2)[:, None, None, None]
    mirror_next = jnp.where(decoder_mask, outputs[::-1], lows[::-1])
    return fwd_next, grad_next, mirror_next
```

```python
import functools

import jax
import jax.numpy as jnp
from jax import lax
from jax.experimental import pallas as pl
from jax.experimental.pallas import tpu as pltpu
from jax.sharding import PartitionSpec as P

BF16 = jnp.bfloat16
F32 = jnp.float32
NN = (((1,), (0,)), ((), ()))
NT = (((1,), (1,)), ((), ()))
MIB = 1 << 20


class Sizes:
    def __init__(self, rows, cols, chan):
        self.rows, self.cols, self.chan = rows, cols, chan


def roles():
    section = lax.axis_index("section")
    sections = lax.axis_size("section")
    row = lax.axis_index("rows")
    decoder = section >= sections // 2
    last = section == sections - 1
    top = row == 0
    bottom = row == lax.axis_size("rows") - 1
    return section, decoder, last, top, bottom


def silu(v):
    return v * jax.nn.sigmoid(v)


def silu_slope(pre):
    sig = jax.nn.sigmoid(pre)
    return sig * (1.0 + pre * (1.0 - sig))


def spread(z, x3, row, value):
    cols, chan = z.cols, z.chan
    count = value.shape[0] // cols
    wide = value.astype(F32).reshape(count, cols, chan)
    col = lax.broadcasted_iota(jnp.int32, wide.shape, 1)
    before = jnp.where(col == 0, 0.0, pltpu.roll(wide, 1, 1))
    after = jnp.where(col == cols - 1, 0.0, pltpu.roll(wide, cols - 1, 1))
    at = slice(row * cols, (row + count) * cols)
    x3[at, 0:chan] = before.reshape(count * cols, chan).astype(BF16)
    x3[at, chan : 2 * chan] = value.astype(BF16)
    x3[at, 2 * chan :] = after.reshape(count * cols, chan).astype(BF16)


def conv(z, x3, pieces, w, acc, flip):
    cols, chan = z.cols, z.chan
    size = sum(n for _, n in pieces) * cols

    def left(a, lanes):
        parts = []
        for start, n in pieces:
            first = (start + a) * cols
            if not isinstance(a, int):
                first = pl.multiple_of(first, cols)
            parts.append(x3[pl.ds(first, n * cols), lanes])
        return parts[0] if len(parts) == 1 else jnp.concatenate(parts, 0)

    def tap_row(a):
        if not flip:
            right = w[pl.ds(3 * a, 3)].reshape(3 * chan, chan)
            return lax.dot_general(left(a, slice(None)), right, NN, preferred_element_type=F32)
        total = None
        for b in range(3):
            right = w[3 * (2 - a) + 2 - b]
            part = lax.dot_general(left(a, slice(b * chan, (b + 1) * chan)), right, NT, preferred_element_type=F32)
            total = part if total is None else total + part
        return total

    for a in range(3):
        if a == 0:
            acc[0:size] = tap_row(0)
        else:
            acc[0:size] += tap_row(a)


def block_input(fwd, held, decoder):
    return fwd.astype(F32) + decoder.astype(F32) * held.astype(F32)


def block_grad(grad, held, decoder):
    return (grad.astype(F32) + (1.0 - decoder.astype(F32)) * held.astype(F32)).astype(BF16)


def halo_body(z, fwd, grad, saved, held, target, up_ref, down_ref, buf, sem):
    rows, cols = z.rows, z.cols
    _, decoder, last, _, _ = roles()
    edge = 4 * cols
    copies = []
    for i, ref in enumerate((fwd, grad, saved, held, target)):
        for e, start in enumerate((0, (rows - 4) * cols)):
            copies.append(pltpu.make_async_copy(ref.at[pl.ds(start, edge)], buf.at[i, e], sem.at[i, e]))
    for c in copies:
        c.start()
    for c in copies:
        c.wait()
    two = 2 * cols
    for e, ref in enumerate((up_ref, down_ref)):
        near = slice(0, two) if e == 0 else slice(two, edge)
        u = block_input(buf[0, e], buf[3, e], decoder).astype(BF16)
        g = block_grad(buf[1, e], buf[3, e], decoder)
        kept = buf[2, e]

        @pl.when(last)
        def _():
            ref[0:edge] = u
            ref[edge:] = buf[4, e][near]

        @pl.when(jnp.logical_not(last))
        def _():
            ref[0:two] = u[near]
            ref[two:edge] = kept[near]
            ref[edge:] = g[near]


def inner_body(z, fwd, grad, saved, held, w1, w2, main_ref, mid_ref, x3, acc, pre):
    rows, cols = z.rows, z.cols
    _, decoder, last, _, _ = roles()
    backward = jnp.logical_and(decoder, jnp.logical_not(last))
    m1, m2 = (rows - 2) * cols, (rows - 4) * cols

    @pl.when(jnp.logical_not(backward))
    def _():
        u = block_input(fwd[...], held[...], decoder)
        spread(z, x3, 0, u.astype(BF16))
        conv(z, x3, [(0, rows - 2)], w1, acc, False)
        mid = silu(acc[0:m1]).astype(BF16)
        mid_ref[...] = mid
        spread(z, x3, 0, mid)
        conv(z, x3, [(0, rows - 4)], w2, acc, False)
        keep = slice(2 * cols, (rows - 2) * cols)
        main_ref[...] = (block_input(fwd[keep], held[keep], decoder) + acc[0:m2]).astype(BF16)

    @pl.when(backward)
    def _():
        spread(z, x3, 0, saved[...])
        conv(z, x3, [(0, rows - 2)], w1, acc, False)
        pre[0:m1] = acc[0:m1]
        spread(z, x3, 0, block_grad(grad[...], held[...], decoder))
        conv(z, x3, [(0, rows - 2)], w2, acc, True)
        mid = (silu_slope(pre[0:m1]) * acc[0:m1]).astype(BF16)
        mid_ref[...] = mid
        spread(z, x3, 0, mid)
        conv(z, x3, [(0, rows - 4)], w1, acc, True)
        keep = slice(2 * cols, (rows - 2) * cols)
        g = block_grad(grad[keep], held[keep], decoder)
        main_ref[...] = (g.astype(F32) + acc[0:m2]).astype(BF16)


def zero_rows(z, value, lo, hi, top, bottom):
    cols = z.cols
    place = lax.broadcasted_iota(jnp.int32, value.shape, 0)
    outside = jnp.logical_or(
        jnp.logical_and(top, place < lo * cols),
        jnp.logical_and(bottom, place >= value.shape[0] - hi * cols),
    )
    return jnp.where(outside, jnp.zeros_like(value), value)


def whole_backward(z, kept, top_grad, w1, w2, x3, acc, pre, out_ref, top, bottom):
    rows, cols = z.rows, z.cols
    m1, m2 = (rows + 2) * cols, rows * cols
    spread(z, x3, 0, kept[...])
    conv(z, x3, [(0, rows + 2)], w1, acc, False)
    pre[0:m1] = acc[0:m1]
    spread(z, x3, 0, top_grad[...])
    conv(z, x3, [(0, rows + 2)], w2, acc, True)
    mid = (silu_slope(pre[0:m1]) * acc[0:m1]).astype(BF16)
    spread(z, x3, 0, zero_rows(z, mid, 1, 1, top, bottom))
    conv(z, x3, [(0, rows)], w1, acc, True)
    out_ref[...] = (top_grad[2 * cols : 2 * cols + m2].astype(F32) + acc[0:m2]).astype(BF16)


def edge_body(z, fwd, grad, saved, held, target, above, below, w1, w2, inner, mid_in, out_ref, x3, acc, pre, kept, top_grad):
    rows, cols = z.rows, z.cols
    two, four, six = 2 * cols, 4 * cols, 6 * cols
    full = rows * cols
    _, decoder, last, top, bottom = roles()
    encoder = jnp.logical_not(decoder)
    m1 = (rows - 2) * cols

    def place_inner():
        out_ref[two : full - two] = inner[...]

    @pl.when(encoder)
    def _():
        place_inner()
        u = block_input(fwd[...], held[...], decoder).astype(BF16)
        spread(z, x3, 0, jnp.concatenate([above[0:two], u[0:two], u[full - two :], below[0:two]], 0))
        conv(z, x3, [(0, 2), (4, 2)], w1, acc, False)
        mid = zero_rows(z, silu(acc[0:four]).astype(BF16), 1, 1, top, bottom)
        spread(z, x3, 0, jnp.concatenate([mid[0:two], mid_in[0:two], mid_in[m1 - two :], mid[two:]], 0))
        conv(z, x3, [(0, 2), (4, 2)], w2, acc, False)
        out_ref[0:two] = (block_input(fwd[0:two], held[0:two], decoder) + acc[0:two]).astype(BF16)
        at = slice(full - two, full)
        out_ref[at] = (block_input(fwd[at], held[at], decoder) + acc[two:four]).astype(BF16)

    @pl.when(jnp.logical_and(decoder, jnp.logical_not(last)))
    def _():
        place_inner()
        at = slice(full - two, full)
        spread(z, x3, 0, jnp.concatenate([above[two:four], saved[0:two], saved[at], below[two:four]], 0))
        conv(z, x3, [(0, 2), (4, 2)], w1, acc, False)
        pre[0:four] = acc[0:four]
        g_low = block_grad(grad[0:two], held[0:two], decoder)
        g_high = block_grad(grad[at], held[at], decoder)
        spread(z, x3, 0, jnp.concatenate([above[four:six], g_low, g_high, below[four:six]], 0))
        conv(z, x3, [(0, 2), (4, 2)], w2, acc, True)
        mid = (silu_slope(pre[0:four]) * acc[0:four]).astype(BF16)
        mid = zero_rows(z, mid, 1, 1, top, bottom)
        spread(z, x3, 0, jnp.concatenate([mid[0:two], mid_in[0:two], mid_in[m1 - two :], mid[two:]], 0))
        conv(z, x3, [(0, 2), (4, 2)], w1, acc, True)
        out_ref[0:two] = (g_low.astype(F32) + acc[0:two]).astype(BF16)
        out_ref[at] = (g_high.astype(F32) + acc[two:four]).astype(BF16)

    @pl.when(last)
    def _():
        eight = 8 * cols
        u = block_input(fwd[...], held[...], decoder)
        ub = u.astype(BF16)
        spread(z, x3, 0, jnp.concatenate([above[0:four], ub[0:two], ub[full - two :], below[0:four]], 0))
        conv(z, x3, [(0, 4), (6, 4)], w1, acc, False)
        mid = zero_rows(z, silu(acc[0:eight]).astype(BF16), 3, 3, top, bottom)
        spread(z, x3, 0, jnp.concatenate([mid[0:four], mid_in[0:two], mid_in[m1 - two :], mid[four:]], 0))
        conv(z, x3, [(0, 4), (6, 4)], w2, acc, False)
        y_low = (jnp.concatenate([above[two:four].astype(F32), u[0:two]], 0) + acc[0:four]).astype(BF16)
        y_high = (jnp.concatenate([u[full - two :], below[0:two].astype(F32)], 0) + acc[four:eight]).astype(BF16)
        y = jnp.concatenate([y_low, inner[...], y_high], 0).astype(F32)
        goal = jnp.concatenate([above[four:six], target[...], below[four:six]], 0).astype(F32)
        top_grad[...] = zero_rows(z, (y - goal).astype(BF16), 2, 2, top, bottom)
        kept[0:two] = above[two:four]
        kept[two : two + full] = ub
        kept[two + full :] = below[0:two]
        whole_backward(z, kept, top_grad, w1, w2, x3, acc, pre, out_ref, top, bottom)


def other_body(z, fwd, grad, saved, held, above, below, w1, w2, out_ref, x3, acc, pre, kept, top_grad):
    rows, cols = z.rows, z.cols
    two, four, six = 2 * cols, 4 * cols, 6 * cols
    full = rows * cols
    _, decoder, last, top, bottom = roles()

    @pl.when(jnp.logical_not(decoder))
    def _():
        kept[0:two] = above[two:four]
        kept[two : two + full] = saved[...]
        kept[two + full :] = below[two:four]
        top_grad[0:two] = above[four:six]
        top_grad[two : two + full] = block_grad(grad[...], held[...], decoder)
        top_grad[two + full :] = below[four:six]
        whole_backward(z, kept, top_grad, w1, w2, x3, acc, pre, out_ref, top, bottom)

    @pl.when(jnp.logical_and(decoder, jnp.logical_not(last)))
    def _():
        spread(z, x3, 0, above[0:two])
        spread(z, x3, 2, block_input(fwd[...], held[...], decoder).astype(BF16))
        spread(z, x3, 2 + rows, below[0:two])
        conv(z, x3, [(0, rows + 2)], w1, acc, False)
        mid = silu(acc[0 : (rows + 2) * cols]).astype(BF16)
        spread(z, x3, 0, zero_rows(z, mid, 1, 1, top, bottom))
        conv(z, x3, [(0, rows)], w2, acc, False)
        out_ref[...] = (block_input(fwd[...], held[...], decoder) + acc[0:full]).astype(BF16)

    @pl.when(last)
    def _():
        out_ref[...] = jnp.zeros_like(out_ref)


def call(body, z, name, args, outs, scratch, spaces, limit, flops=0, moved=0):
    return pl.pallas_call(
        functools.partial(body, z),
        out_shape=[jax.ShapeDtypeStruct(s, BF16) for s in outs],
        in_specs=[pl.BlockSpec(memory_space=s) for s in spaces],
        out_specs=[pl.BlockSpec(memory_space=pltpu.VMEM) for _ in outs],
        scratch_shapes=scratch,
        compiler_params=pltpu.CompilerParams(vmem_limit_bytes=limit),
        cost_estimate=pl.CostEstimate(flops=flops, bytes_accessed=moved, transcendentals=0),
        name=name,
    )(*args)


def chain_pairs(count):
    half = count // 2
    near, relay, second = [], [], []
    for s in range(half):
        mirror = count - 1 - s
        if s % 2 == 0:
            near += [(s, s + 1), (mirror, mirror - 1)]
        elif s + 1 < half:
            relay += [(mirror, s + 1), (s, mirror - 1)]
        if s >= 1:
            second += [(s, s - 1), (mirror, mirror + 1)]
    return near, relay, second


def on_device(fwd_in, grad_in, saved_in, mirror_held, target, w_first, w_second):
    shape = fwd_in.shape[1:]
    rows, cols, chan = shape
    z = Sizes(rows, cols, chan)
    flat = lambda v: v.reshape(rows * cols, chan)
    fwd, grad, saved, held = (flat(v[0]) for v in (fwd_in, grad_in, saved_in, mirror_held))
    goal = flat(target)
    w1 = w_first[0].reshape(9, chan, chan)
    w2 = w_second[0].reshape(9, chan, chan)
    sections = lax.axis_size("section")
    section, decoder, last, _, _ = roles()
    any_, vm = pl.ANY, pltpu.VMEM
    six = (6 * cols, chan)

    to_up, to_down = call(
        halo_body, z, "halo", (fwd, grad, saved, held, goal), (six, six),
        [pltpu.VMEM((5, 2, 4 * cols, chan), BF16), pltpu.SemaphoreType.DMA((5, 2))],
        [any_] * 5, 8 * MIB,
    )
    count = lax.axis_size("rows")
    below = lax.ppermute(to_up, "rows", [(i + 1, i) for i in range(count - 1)])
    above = lax.ppermute(to_down, "rows", [(i, i + 1) for i in range(count - 1)])

    x3 = pltpu.VMEM(((rows + 4) * cols, 3 * chan), BF16)
    acc = pltpu.VMEM(((rows + 2) * cols, chan), F32)
    wide = pltpu.VMEM(((rows + 4) * cols, chan), BF16)
    row_flops = 2 * cols * 9 * chan * chan
    main, mid = call(
        inner_body, z, "inner", (fwd, grad, saved, held, w1, w2),
        (((rows - 4) * cols, chan), ((rows - 2) * cols, chan)),
        [x3, acc, acc], [vm] * 6, 24 * MIB, 40 * row_flops, 12 * MIB,
    )
    (first,) = call(
        edge_body, z, "edge", (fwd, grad, saved, held, goal, above, below, w1, w2, main, mid),
        ((rows * cols, chan),), [x3, acc, acc, wide, wide], [vm] * 11, 24 * MIB, 24 * row_flops, 12 * MIB,
    )
    near_pairs, relay_pairs, second_pairs = chain_pairs(sections)
    mirrored = lax.ppermute(first, "section", [(s, sections - 1 - s) for s in range(sections)])
    near = lax.ppermute(first, "section", near_pairs)
    (second,) = call(
        other_body, z, "other", (fwd, grad, saved, held, above, below, w1, w2),
        ((rows * cols, chan),), [x3, acc, acc, wide, wide], [vm] * 8, 24 * MIB, 52 * row_flops, 12 * MIB,
    )
    turned = lax.ppermute(second, "section", second_pairs)
    relayed = lax.ppermute(mirrored, "section", relay_pairs)
    half = sections // 2
    onward = jnp.where(section % 2 == (1 - decoder.astype(jnp.int32)), near, relayed)
    inward = jnp.where(jnp.logical_or(section == half, section == half - 1), mirrored, turned)
    fwd_next = jnp.where(decoder, inward, onward)
    grad_next = jnp.where(decoder, onward, inward)
    full = lambda v: v.reshape((1,) + shape)
    return full(fwd_next), full(grad_next), full(mirrored)


def solution(mesh):
    maps = P("section", "rows", None, None)
    weights = P("section", None, None, None, None)
    return jax.shard_map(
        on_device,
        mesh=mesh,
        in_specs=(maps, maps, maps, maps, P("rows", None, None), weights, weights),
        out_specs=(maps, maps, maps),
        check_vma=False,
    )
```

```python
import functools

import jax
import jax.numpy as jnp
from jax import lax
from jax.experimental import pallas as pl
from jax.experimental.pallas import tpu as pltpu
from jax.sharding import PartitionSpec as P

BF16 = jnp.bfloat16
F32 = jnp.float32
NN = (((1,), (0,)), ((), ()))
NT = (((1,), (1,)), ((), ()))
MIB = 1 << 20


class Sizes:
    def __init__(self, rows, cols, chan):
        self.rows, self.cols, self.chan = rows, cols, chan


def roles():
    section = lax.axis_index("section")
    sections = lax.axis_size("section")
    row = lax.axis_index("rows")
    decoder = section >= sections // 2
    last = section == sections - 1
    top = row == 0
    bottom = row == lax.axis_size("rows") - 1
    return section, decoder, last, top, bottom


def silu(v):
    return v * jax.nn.sigmoid(v)


def silu_slope(pre):
    sig = jax.nn.sigmoid(pre)
    return sig * (1.0 + pre * (1.0 - sig))


def spread(z, x3, row, value):
    cols, chan = z.cols, z.chan
    count = value.shape[0] // cols
    wide = value.astype(F32).reshape(count, cols, chan)
    col = lax.broadcasted_iota(jnp.int32, wide.shape, 1)
    before = jnp.where(col == 0, 0.0, pltpu.roll(wide, 1, 1))
    after = jnp.where(col == cols - 1, 0.0, pltpu.roll(wide, cols - 1, 1))
    at = slice(row * cols, (row + count) * cols)
    x3[at, 0:chan] = before.reshape(count * cols, chan).astype(BF16)
    x3[at, chan : 2 * chan] = value.astype(BF16)
    x3[at, 2 * chan :] = after.reshape(count * cols, chan).astype(BF16)


def conv(z, x3, pieces, w, acc, flip):
    cols, chan = z.cols, z.chan
    size = sum(n for _, n in pieces) * cols

    def left(a, lanes):
        parts = []
        for start, n in pieces:
            first = (start + a) * cols
            if not isinstance(a, int):
                first = pl.multiple_of(first, cols)
            parts.append(x3[pl.ds(first, n * cols), lanes])
        return parts[0] if len(parts) == 1 else jnp.concatenate(parts, 0)

    def tap_row(a):
        if not flip:
            right = w[pl.ds(3 * a, 3)].reshape(3 * chan, chan)
            return lax.dot_general(left(a, slice(None)), right, NN, preferred_element_type=F32)
        total = None
        for b in range(3):
            right = w[3 * (2 - a) + 2 - b]
            part = lax.dot_general(left(a, slice(b * chan, (b + 1) * chan)), right, NT, preferred_element_type=F32)
            total = part if total is None else total + part
        return total

    for a in range(3):
        if a == 0:
            acc[0:size] = tap_row(0)
        else:
            acc[0:size] += tap_row(a)


def block_input(fwd, held, decoder):
    return fwd.astype(F32) + decoder.astype(F32) * held.astype(F32)


def block_grad(grad, held, decoder):
    return (grad.astype(F32) + (1.0 - decoder.astype(F32)) * held.astype(F32)).astype(BF16)


def halo_body(z, fwd, grad, saved, held, target, up_ref, down_ref, buf, sem):
    rows, cols = z.rows, z.cols
    _, decoder, last, _, _ = roles()
    edge = 4 * cols
    copies = []
    for i, ref in enumerate((fwd, grad, saved, held, target)):
        for e, start in enumerate((0, (rows - 4) * cols)):
            copies.append(pltpu.make_async_copy(ref.at[pl.ds(start, edge)], buf.at[i, e], sem.at[i, e]))
    for c in copies:
        c.start()
    for c in copies:
        c.wait()
    two = 2 * cols
    for e, ref in enumerate((up_ref, down_ref)):
        near = slice(0, two) if e == 0 else slice(two, edge)
        u = block_input(buf[0, e], buf[3, e], decoder).astype(BF16)
        g = block_grad(buf[1, e], buf[3, e], decoder)
        kept = buf[2, e]

        @pl.when(last)
        def _():
            ref[0:edge] = u
            ref[edge:] = buf[4, e][near]

        @pl.when(jnp.logical_not(last))
        def _():
            ref[0:two] = u[near]
            ref[two:edge] = kept[near]
            ref[edge:] = g[near]


def inner_body(z, fwd, grad, saved, held, w1, w2, main_ref, mid_ref, x3, acc, pre):
    rows, cols = z.rows, z.cols
    _, decoder, last, _, _ = roles()
    backward = jnp.logical_and(decoder, jnp.logical_not(last))
    m1, m2 = (rows - 2) * cols, (rows - 4) * cols

    @pl.when(jnp.logical_not(backward))
    def _():
        u = block_input(fwd[...], held[...], decoder)
        spread(z, x3, 0, u.astype(BF16))
        conv(z, x3, [(0, rows - 2)], w1, acc, False)
        mid = silu(acc[0:m1]).astype(BF16)
        mid_ref[...] = mid
        spread(z, x3, 0, mid)
        conv(z, x3, [(0, rows - 4)], w2, acc, False)
        keep = slice(2 * cols, (rows - 2) * cols)
        main_ref[...] = (block_input(fwd[keep], held[keep], decoder) + acc[0:m2]).astype(BF16)

    @pl.when(backward)
    def _():
        spread(z, x3, 0, saved[...])
        conv(z, x3, [(0, rows - 2)], w1, acc, False)
        pre[0:m1] = acc[0:m1]
        spread(z, x3, 0, block_grad(grad[...], held[...], decoder))
        conv(z, x3, [(0, rows - 2)], w2, acc, True)
        mid = (silu_slope(pre[0:m1]) * acc[0:m1]).astype(BF16)
        mid_ref[...] = mid
        spread(z, x3, 0, mid)
        conv(z, x3, [(0, rows - 4)], w1, acc, True)
        keep = slice(2 * cols, (rows - 2) * cols)
        g = block_grad(grad[keep], held[keep], decoder)
        main_ref[...] = (g.astype(F32) + acc[0:m2]).astype(BF16)


def zero_rows(z, value, lo, hi, top, bottom):
    cols = z.cols
    place = lax.broadcasted_iota(jnp.int32, value.shape, 0)
    outside = jnp.logical_or(
        jnp.logical_and(top, place < lo * cols),
        jnp.logical_and(bottom, place >= value.shape[0] - hi * cols),
    )
    return jnp.where(outside, jnp.zeros_like(value), value)


def whole_backward(z, kept, top_grad, w1, w2, x3, acc, pre, out_ref, top, bottom):
    rows, cols = z.rows, z.cols
    m1, m2 = (rows + 2) * cols, rows * cols
    spread(z, x3, 0, kept[...])
    conv(z, x3, [(0, rows + 2)], w1, acc, False)
    pre[0:m1] = acc[0:m1]
    spread(z, x3, 0, top_grad[...])
    conv(z, x3, [(0, rows + 2)], w2, acc, True)
    mid = (silu_slope(pre[0:m1]) * acc[0:m1]).astype(BF16)
    spread(z, x3, 0, zero_rows(z, mid, 1, 1, top, bottom))
    conv(z, x3, [(0, rows)], w1, acc, True)
    out_ref[...] = (top_grad[2 * cols : 2 * cols + m2].astype(F32) + acc[0:m2]).astype(BF16)


def edge_body(z, fwd, grad, saved, held, target, above, below, w1, w2, inner, mid_in, out_ref, x3, acc, pre, kept, top_grad):
    rows, cols = z.rows, z.cols
    two, four, six = 2 * cols, 4 * cols, 6 * cols
    full = rows * cols
    _, decoder, last, top, bottom = roles()
    encoder = jnp.logical_not(decoder)
    m1 = (rows - 2) * cols

    def place_inner():
        out_ref[two : full - two] = inner[...]

    @pl.when(encoder)
    def _():
        place_inner()
        u = block_input(fwd[...], held[...], decoder).astype(BF16)
        spread(z, x3, 0, jnp.concatenate([above[0:two], u[0:two], u[full - two :], below[0:two]], 0))
        conv(z, x3, [(0, 2), (4, 2)], w1, acc, False)
        mid = zero_rows(z, silu(acc[0:four]).astype(BF16), 1, 1, top, bottom)
        spread(z, x3, 0, jnp.concatenate([mid[0:two], mid_in[0:two], mid_in[m1 - two :], mid[two:]], 0))
        conv(z, x3, [(0, 2), (4, 2)], w2, acc, False)
        out_ref[0:two] = (block_input(fwd[0:two], held[0:two], decoder) + acc[0:two]).astype(BF16)
        at = slice(full - two, full)
        out_ref[at] = (block_input(fwd[at], held[at], decoder) + acc[two:four]).astype(BF16)

    @pl.when(jnp.logical_and(decoder, jnp.logical_not(last)))
    def _():
        place_inner()
        at = slice(full - two, full)
        spread(z, x3, 0, jnp.concatenate([above[two:four], saved[0:two], saved[at], below[two:four]], 0))
        conv(z, x3, [(0, 2), (4, 2)], w1, acc, False)
        pre[0:four] = acc[0:four]
        g_low = block_grad(grad[0:two], held[0:two], decoder)
        g_high = block_grad(grad[at], held[at], decoder)
        spread(z, x3, 0, jnp.concatenate([above[four:six], g_low, g_high, below[four:six]], 0))
        conv(z, x3, [(0, 2), (4, 2)], w2, acc, True)
        mid = (silu_slope(pre[0:four]) * acc[0:four]).astype(BF16)
        mid = zero_rows(z, mid, 1, 1, top, bottom)
        spread(z, x3, 0, jnp.concatenate([mid[0:two], mid_in[0:two], mid_in[m1 - two :], mid[two:]], 0))
        conv(z, x3, [(0, 2), (4, 2)], w1, acc, True)
        out_ref[0:two] = (g_low.astype(F32) + acc[0:two]).astype(BF16)
        out_ref[at] = (g_high.astype(F32) + acc[two:four]).astype(BF16)

    @pl.when(last)
    def _():
        eight = 8 * cols
        u = block_input(fwd[...], held[...], decoder)
        ub = u.astype(BF16)
        spread(z, x3, 0, jnp.concatenate([above[0:four], ub[0:two], ub[full - two :], below[0:four]], 0))
        conv(z, x3, [(0, 4), (6, 4)], w1, acc, False)
        mid = zero_rows(z, silu(acc[0:eight]).astype(BF16), 3, 3, top, bottom)
        spread(z, x3, 0, jnp.concatenate([mid[0:four], mid_in[0:two], mid_in[m1 - two :], mid[four:]], 0))
        conv(z, x3, [(0, 4), (6, 4)], w2, acc, False)
        y_low = (jnp.concatenate([above[two:four].astype(F32), u[0:two]], 0) + acc[0:four]).astype(BF16)
        y_high = (jnp.concatenate([u[full - two :], below[0:two].astype(F32)], 0) + acc[four:eight]).astype(BF16)
        y = jnp.concatenate([y_low, inner[...], y_high], 0).astype(F32)
        goal = jnp.concatenate([above[four:six], target[...], below[four:six]], 0).astype(F32)
        top_grad[...] = zero_rows(z, (y - goal).astype(BF16), 2, 2, top, bottom)
        kept[0:two] = above[two:four]
        kept[two : two + full] = ub
        kept[two + full :] = below[0:two]
        whole_backward(z, kept, top_grad, w1, w2, x3, acc, pre, out_ref, top, bottom)


def other_body(z, fwd, grad, saved, held, above, below, w1, w2, out_ref, x3, acc, pre, kept, top_grad):
    rows, cols = z.rows, z.cols
    two, four, six = 2 * cols, 4 * cols, 6 * cols
    full = rows * cols
    _, decoder, last, top, bottom = roles()

    @pl.when(jnp.logical_not(decoder))
    def _():
        kept[0:two] = above[two:four]
        kept[two : two + full] = saved[...]
        kept[two + full :] = below[two:four]
        top_grad[0:two] = above[four:six]
        top_grad[two : two + full] = block_grad(grad[...], held[...], decoder)
        top_grad[two + full :] = below[four:six]
        whole_backward(z, kept, top_grad, w1, w2, x3, acc, pre, out_ref, top, bottom)

    @pl.when(jnp.logical_and(decoder, jnp.logical_not(last)))
    def _():
        spread(z, x3, 0, above[0:two])
        spread(z, x3, 2, block_input(fwd[...], held[...], decoder).astype(BF16))
        spread(z, x3, 2 + rows, below[0:two])
        conv(z, x3, [(0, rows + 2)], w1, acc, False)
        mid = silu(acc[0 : (rows + 2) * cols]).astype(BF16)
        spread(z, x3, 0, zero_rows(z, mid, 1, 1, top, bottom))
        conv(z, x3, [(0, rows)], w2, acc, False)
        out_ref[...] = (block_input(fwd[...], held[...], decoder) + acc[0:full]).astype(BF16)

    @pl.when(last)
    def _():
        out_ref[...] = jnp.zeros_like(out_ref)


def call(body, z, name, args, outs, scratch, spaces, limit, flops=0, moved=0):
    return pl.pallas_call(
        functools.partial(body, z),
        out_shape=[jax.ShapeDtypeStruct(s, BF16) for s in outs],
        in_specs=[pl.BlockSpec(memory_space=s) for s in spaces],
        out_specs=[pl.BlockSpec(memory_space=pltpu.VMEM) for _ in outs],
        scratch_shapes=scratch,
        compiler_params=pltpu.CompilerParams(vmem_limit_bytes=limit),
        cost_estimate=pl.CostEstimate(flops=flops, bytes_accessed=moved, transcendentals=0),
        name=name,
    )(*args)


def chain_pairs(count):
    half = count // 2
    near, relay, second = [], [], []
    for s in range(half):
        mirror = count - 1 - s
        if s % 2 == 0:
            near += [(s, s + 1), (mirror, mirror - 1)]
        elif s + 1 < half:
            relay += [(mirror, s + 1), (s, mirror - 1)]
        if s >= 1:
            second += [(s, s - 1), (mirror, mirror + 1)]
    return near, relay, second


def on_device(fwd_in, grad_in, saved_in, mirror_held, target, w_first, w_second):
    shape = fwd_in.shape[1:]
    rows, cols, chan = shape
    z = Sizes(rows, cols, chan)
    flat = lambda v: v.reshape(rows * cols, chan)
    fwd, grad, saved, held = (flat(v[0]) for v in (fwd_in, grad_in, saved_in, mirror_held))
    goal = flat(target)
    w1 = w_first[0].reshape(9, chan, chan)
    w2 = w_second[0].reshape(9, chan, chan)
    sections = lax.axis_size("section")
    section, decoder, last, _, _ = roles()
    any_, vm = pltpu.HBM, pltpu.VMEM
    six = (6 * cols, chan)

    to_up, to_down = call(
        halo_body, z, "halo", tuple(pltpu.with_memory_space_constraint(v, pltpu.HBM) for v in (fwd, grad, saved, held, goal)), (six, six),
        [pltpu.VMEM((5, 2, 4 * cols, chan), BF16), pltpu.SemaphoreType.DMA((5, 2))],
        [any_] * 5, 8 * MIB, 6_000_000_000, 0,
    )
    count = lax.axis_size("rows")
    below = lax.ppermute(to_up, "rows", [(i + 1, i) for i in range(count - 1)])
    above = lax.ppermute(to_down, "rows", [(i, i + 1) for i in range(count - 1)])

    x3 = pltpu.VMEM(((rows + 4) * cols, 3 * chan), BF16)
    acc = pltpu.VMEM(((rows + 2) * cols, chan), F32)
    wide = pltpu.VMEM(((rows + 4) * cols, chan), BF16)
    row_flops = 2 * cols * 9 * chan * chan
    main, mid = call(
        inner_body, z, "inner", (fwd, grad, saved, held, w1, w2),
        (((rows - 4) * cols, chan), ((rows - 2) * cols, chan)),
        [x3, acc, acc], [vm] * 6, 24 * MIB, 40 * row_flops, 12 * MIB,
    )
    (first,) = call(
        edge_body, z, "edge", (fwd, grad, saved, held, goal, above, below, w1, w2, main, mid),
        ((rows * cols, chan),), [x3, acc, acc, wide, wide], [vm] * 11, 24 * MIB, 24 * row_flops, 12 * MIB,
    )
    near_pairs, relay_pairs, second_pairs = chain_pairs(sections)
    mirrored = lax.ppermute(first, "section", [(s, sections - 1 - s) for s in range(sections)])
    near = lax.ppermute(first, "section", near_pairs)
    (second,) = call(
        other_body, z, "other", (fwd, grad, saved, held, above, below, w1, w2),
        ((rows * cols, chan),), [x3, acc, acc, wide, wide], [vm] * 8, 24 * MIB, 52 * row_flops, 12 * MIB,
    )
    turned = lax.ppermute(second, "section", second_pairs)
    relayed = lax.ppermute(mirrored, "section", relay_pairs)
    half = sections // 2
    onward = jnp.where(section % 2 == (1 - decoder.astype(jnp.int32)), near, relayed)
    inward = jnp.where(jnp.logical_or(section == half, section == half - 1), mirrored, turned)
    fwd_next = jnp.where(decoder, inward, onward)
    grad_next = jnp.where(decoder, onward, inward)
    full = lambda v: v.reshape((1,) + shape)
    return full(fwd_next), full(grad_next), full(mirrored)


def solution(mesh):
    maps = P("section", "rows", None, None)
    weights = P("section", None, None, None, None)
    return jax.shard_map(
        on_device,
        mesh=mesh,
        in_specs=(maps, maps, maps, maps, P("rows", None, None), weights, weights),
        out_specs=(maps, maps, maps),
        check_vma=False,
    )
```

```python
import functools

import jax
import jax.numpy as jnp
from jax import lax
from jax.experimental import pallas as pl
from jax.experimental.pallas import tpu as pltpu
from jax.sharding import PartitionSpec as P


BF16 = jnp.bfloat16
F32 = jnp.float32
NN = (((1,), (0,)), ((), ()))
NT = (((1,), (1,)), ((), ()))
MIB = 1 << 20


class Sizes:
    def __init__(self, rows, cols, chan):
        self.rows, self.cols, self.chan = rows, cols, chan


def roles():
    section = lax.axis_index("section")
    sections = lax.axis_size("section")
    row = lax.axis_index("rows")
    decoder = section >= sections // 2
    last = section == sections - 1
    top = row == 0
    bottom = row == lax.axis_size("rows") - 1
    return section, decoder, last, top, bottom


def silu(v):
    return v * jax.nn.sigmoid(v)


def silu_slope(pre):
    sig = jax.nn.sigmoid(pre)
    return sig * (1.0 + pre * (1.0 - sig))


def spread(z, x3, row, value):
    cols, chan = z.cols, z.chan
    count = value.shape[0] // cols
    wide = value.astype(F32).reshape(count, cols, chan)
    col = lax.broadcasted_iota(jnp.int32, wide.shape, 1)
    before = jnp.where(col == 0, 0.0, pltpu.roll(wide, 1, 1))
    after = jnp.where(col == cols - 1, 0.0, pltpu.roll(wide, cols - 1, 1))
    at = slice(row * cols, (row + count) * cols)
    x3[at, 0:chan] = before.reshape(count * cols, chan).astype(BF16)
    x3[at, chan : 2 * chan] = value.astype(BF16)
    x3[at, 2 * chan :] = after.reshape(count * cols, chan).astype(BF16)


def conv(z, x3, pieces, w, acc, flip):
    cols, chan = z.cols, z.chan
    size = sum(n for _, n in pieces) * cols

    def left(a, lanes):
        parts = []
        for start, n in pieces:
            first = (start + a) * cols
            if not isinstance(a, int):
                first = pl.multiple_of(first, cols)
            parts.append(x3[pl.ds(first, n * cols), lanes])
        return parts[0] if len(parts) == 1 else jnp.concatenate(parts, 0)

    def tap_row(a):
        if not flip:
            right = w[pl.ds(3 * a, 3)].reshape(3 * chan, chan)
            return lax.dot_general(left(a, slice(None)), right, NN, preferred_element_type=F32)
        total = None
        for b in range(3):
            right = w[3 * (2 - a) + 2 - b]
            part = lax.dot_general(left(a, slice(b * chan, (b + 1) * chan)), right, NT, preferred_element_type=F32)
            total = part if total is None else total + part
        return total

    for a in range(3):
        if a == 0:
            acc[0:size] = tap_row(0)
        else:
            acc[0:size] += tap_row(a)


def block_input(fwd, held, decoder):
    return fwd.astype(F32) + decoder.astype(F32) * held.astype(F32)


def block_grad(grad, held, decoder):
    return (grad.astype(F32) + (1.0 - decoder.astype(F32)) * held.astype(F32)).astype(BF16)


def halo_body(z, fwd, grad, saved, held, target, up_ref, down_ref, buf, sem):
    rows, cols = z.rows, z.cols
    _, decoder, last, _, _ = roles()
    edge = 4 * cols
    copies = []
    for i, ref in enumerate((fwd, grad, saved, held, target)):
        for e, start in enumerate((0, (rows - 4) * cols)):
            copies.append(pltpu.make_async_copy(ref.at[pl.ds(start, edge)], buf.at[i, e], sem.at[i, e]))
    for c in copies:
        c.start()
    for c in copies:
        c.wait()
    two = 2 * cols
    for e, ref in enumerate((up_ref, down_ref)):
        near = slice(0, two) if e == 0 else slice(two, edge)
        u = block_input(buf[0, e], buf[3, e], decoder).astype(BF16)
        g = block_grad(buf[1, e], buf[3, e], decoder)
        kept = buf[2, e]

        @pl.when(last)
        def _():
            ref[0:edge] = u
            ref[edge:] = buf[4, e][near]

        @pl.when(jnp.logical_not(last))
        def _():
            ref[0:two] = u[near]
            ref[two:edge] = kept[near]
            ref[edge:] = g[near]


def inner_forward(z, fwd, held, w1, w2, main_ref, mid_ref, x3, acc):
    rows, cols = z.rows, z.cols
    _, decoder, last, _, _ = roles()
    m1, m2 = (rows - 2) * cols, (rows - 4) * cols

    @pl.when(jnp.logical_or(jnp.logical_not(decoder), last))
    def _():
        u = block_input(fwd[...], held[...], decoder)
        spread(z, x3, 0, u.astype(BF16))
        conv(z, x3, [(0, rows - 2)], w1, acc, False)
        mid = silu(acc[0:m1]).astype(BF16)
        mid_ref[...] = mid
        spread(z, x3, 0, mid)
        conv(z, x3, [(0, rows - 4)], w2, acc, False)
        keep = slice(2 * cols, (rows - 2) * cols)
        main_ref[...] = (block_input(fwd[keep], held[keep], decoder) + acc[0:m2]).astype(BF16)


def inner_backward(z, grad, saved, held, w1, w2, main_ref, mid_ref, x3, acc, pre):
    rows, cols = z.rows, z.cols
    _, decoder, last, _, _ = roles()
    m1, m2 = (rows - 2) * cols, (rows - 4) * cols

    @pl.when(jnp.logical_and(decoder, jnp.logical_not(last)))
    def _():
        spread(z, x3, 0, saved[...])
        conv(z, x3, [(0, rows - 2)], w1, acc, False)
        pre[0:m1] = acc[0:m1]
        spread(z, x3, 0, block_grad(grad[...], held[...], decoder))
        conv(z, x3, [(0, rows - 2)], w2, acc, True)
        mid = (silu_slope(pre[0:m1]) * acc[0:m1]).astype(BF16)
        mid_ref[...] = mid
        spread(z, x3, 0, mid)
        conv(z, x3, [(0, rows - 4)], w1, acc, True)
        keep = slice(2 * cols, (rows - 2) * cols)
        g = block_grad(grad[keep], held[keep], decoder)
        main_ref[...] = (g.astype(F32) + acc[0:m2]).astype(BF16)


def zero_rows(z, value, lo, hi, top, bottom):
    cols = z.cols
    place = lax.broadcasted_iota(jnp.int32, value.shape, 0)
    outside = jnp.logical_or(
        jnp.logical_and(top, place < lo * cols),
        jnp.logical_and(bottom, place >= value.shape[0] - hi * cols),
    )
    return jnp.where(outside, jnp.zeros_like(value), value)


def whole_backward(z, kept, top_grad, w1, w2, x3, acc, pre, out_ref, top, bottom):
    rows, cols = z.rows, z.cols
    m1, m2 = (rows + 2) * cols, rows * cols
    spread(z, x3, 0, kept[...])
    conv(z, x3, [(0, rows + 2)], w1, acc, False)
    pre[0:m1] = acc[0:m1]
    spread(z, x3, 0, top_grad[...])
    conv(z, x3, [(0, rows + 2)], w2, acc, True)
    mid = (silu_slope(pre[0:m1]) * acc[0:m1]).astype(BF16)
    spread(z, x3, 0, zero_rows(z, mid, 1, 1, top, bottom))
    conv(z, x3, [(0, rows)], w1, acc, True)
    out_ref[...] = (top_grad[2 * cols : 2 * cols + m2].astype(F32) + acc[0:m2]).astype(BF16)


def rest_body(
    z, fwd, grad, saved, held, target, above, below, w1, w2, y_inner, y_mid, g_inner, g_mid,
    first_ref, rim_ref, second_ref, x3, acc, pre, kept, top_grad,
):
    rows, cols = z.rows, z.cols
    two, four, six, eight = 2 * cols, 4 * cols, 6 * cols, 8 * cols
    full = rows * cols
    section, decoder, last, top, bottom = roles()
    encoder = jnp.logical_not(decoder)
    decoder_only = decoder & jnp.logical_not(last)
    closing = last
    m1 = (rows - 2) * cols
    high = slice(full - two, full)

    @pl.when(encoder)
    def _():
        first_ref[two : full - two] = y_inner[...]
        u = block_input(fwd[...], held[...], decoder).astype(BF16)
        spread(z, x3, 0, jnp.concatenate([above[0:two], u[0:two], u[full - two :], below[0:two]], 0))
        conv(z, x3, [(0, 2), (4, 2)], w1, acc, False)
        mid = zero_rows(z, silu(acc[0:four]).astype(BF16), 1, 1, top, bottom)
        spread(z, x3, 0, jnp.concatenate([mid[0:two], y_mid[0:two], y_mid[m1 - two :], mid[two:]], 0))
        conv(z, x3, [(0, 2), (4, 2)], w2, acc, False)
        first_ref[0:two] = (block_input(fwd[0:two], held[0:two], decoder) + acc[0:two]).astype(BF16)
        first_ref[high] = (block_input(fwd[high], held[high], decoder) + acc[two:four]).astype(BF16)
        kept[0:two] = above[two:four]
        kept[two : two + full] = saved[...]
        kept[two + full :] = below[two:four]
        top_grad[0:two] = above[four:six]
        top_grad[two : two + full] = block_grad(grad[...], held[...], decoder)
        top_grad[two + full :] = below[four:six]

    @pl.when(closing)
    def _():
        u = block_input(fwd[...], held[...], decoder)
        ub = u.astype(BF16)
        spread(z, x3, 0, jnp.concatenate([above[0:four], ub[0:two], ub[full - two :], below[0:four]], 0))
        conv(z, x3, [(0, 4), (6, 4)], w1, acc, False)
        mid = zero_rows(z, silu(acc[0:eight]).astype(BF16), 3, 3, top, bottom)
        spread(z, x3, 0, jnp.concatenate([mid[0:four], y_mid[0:two], y_mid[m1 - two :], mid[four:]], 0))
        conv(z, x3, [(0, 4), (6, 4)], w2, acc, False)
        y_low = (jnp.concatenate([above[two:four].astype(F32), u[0:two]], 0) + acc[0:four]).astype(BF16)
        y_high = (jnp.concatenate([u[full - two :], below[0:two].astype(F32)], 0) + acc[four:eight]).astype(BF16)
        y = jnp.concatenate([y_low, y_inner[...], y_high], 0).astype(F32)
        goal = jnp.concatenate([above[four:six], target[...], below[four:six]], 0).astype(F32)
        top_grad[...] = zero_rows(z, (y - goal).astype(BF16), 2, 2, top, bottom)
        kept[0:two] = above[two:four]
        kept[two : two + full] = ub
        kept[two + full :] = below[0:two]

    @pl.when((encoder & (section != 0)) | closing)
    def _():
        whole_backward(z, kept, top_grad, w1, w2, x3, acc, pre, second_ref, top, bottom)

    @pl.when(closing)
    def _():
        first_ref[...] = second_ref[...]

    @pl.when(decoder_only)
    def _():
        first_ref[two : full - two] = g_inner[...]
        spread(z, x3, 0, jnp.concatenate([above[two:four], saved[0:two], saved[high], below[two:four]], 0))
        conv(z, x3, [(0, 2), (4, 2)], w1, acc, False)
        pre[0:four] = acc[0:four]
        g_low = block_grad(grad[0:two], held[0:two], decoder)
        g_high = block_grad(grad[high], held[high], decoder)
        spread(z, x3, 0, jnp.concatenate([above[four:six], g_low, g_high, below[four:six]], 0))
        conv(z, x3, [(0, 2), (4, 2)], w2, acc, True)
        mid = (silu_slope(pre[0:four]) * acc[0:four]).astype(BF16)
        mid = zero_rows(z, mid, 1, 1, top, bottom)
        spread(z, x3, 0, jnp.concatenate([mid[0:two], g_mid[0:two], g_mid[m1 - two :], mid[two:]], 0))
        conv(z, x3, [(0, 2), (4, 2)], w1, acc, True)
        first_ref[0:two] = (g_low.astype(F32) + acc[0:two]).astype(BF16)
        first_ref[high] = (g_high.astype(F32) + acc[two:four]).astype(BF16)

        spread(z, x3, 0, above[0:two])
        spread(z, x3, 2, block_input(fwd[...], held[...], decoder).astype(BF16))
        spread(z, x3, 2 + rows, below[0:two])
        conv(z, x3, [(0, rows + 2)], w1, acc, False)
        hidden = silu(acc[0 : (rows + 2) * cols]).astype(BF16)
        spread(z, x3, 0, zero_rows(z, hidden, 1, 1, top, bottom))
        conv(z, x3, [(0, rows)], w2, acc, False)
        second_ref[...] = (block_input(fwd[...], held[...], decoder) + acc[0:full]).astype(BF16)

    rim_ref[0:two] = first_ref[0:two]
    rim_ref[two:] = first_ref[full - two :]

    @pl.when(section == 1)
    def _():
        first_ref[...] = second_ref[...]


def mirror_body(z, to_decoder, to_encoder, rim, out_ref, sem):
    two, full = 2 * z.cols, z.rows * z.cols
    _, decoder, _, _, _ = roles()
    lower = pltpu.make_async_copy(rim.at[pl.ds(0, two)], out_ref.at[pl.ds(0, two)], sem.at[0])
    upper = pltpu.make_async_copy(rim.at[pl.ds(two, two)], out_ref.at[pl.ds(full - two, two)], sem.at[1])
    lower.start()
    upper.start()
    for here, source in ((decoder, to_decoder), (jnp.logical_not(decoder), to_encoder)):

        @pl.when(here)
        def _():
            copy = pltpu.make_async_copy(source, out_ref.at[pl.ds(two, full - 2 * two)], sem.at[2])
            copy.start()
            copy.wait()

    lower.wait()
    upper.wait()


def pick_body(z, to_decoder, to_encoder, out_ref):
    _, decoder, _, _, _ = roles()

    @pl.when(decoder)
    def _():
        out_ref[...] = to_decoder[...]

    @pl.when(jnp.logical_not(decoder))
    def _():
        out_ref[...] = to_encoder[...]


def finish_body(
    z, near, to_decoder, to_encoder, rim, relay_inner, relay_rim, turned, mirror_in, fwd_ref, grad_ref, mirror_ref, sem
):
    two, full = 2 * z.cols, z.rows * z.cols
    section, decoder, _, _, _ = roles()
    half = lax.axis_size("section") // 2
    plain = section % 2 == 1 - decoder.astype(jnp.int32)
    joined = (section == half) | (section == half - 1)
    first_one = section == 0
    over = jnp.logical_not(joined | first_one)

    def pieces(ref, main, edges, base):
        return [
            pltpu.make_async_copy(main, ref.at[pl.ds(two, full - 2 * two)], sem.at[base]),
            pltpu.make_async_copy(edges.at[pl.ds(0, two)], ref.at[pl.ds(0, two)], sem.at[base + 1]),
            pltpu.make_async_copy(edges.at[pl.ds(two, two)], ref.at[pl.ds(full - two, two)], sem.at[base + 2]),
        ]

    def run(here, copies):
        @pl.when(here)
        def _():
            made = copies()
            for c in made:
                c.start()
            for c in made:
                c.wait()

    for is_decoder in (False, True):
        onward, inward = (grad_ref, fwd_ref) if is_decoder else (fwd_ref, grad_ref)
        inner = to_decoder if is_decoder else to_encoder
        here = decoder == is_decoder
        run(here & plain & joined, lambda: [pltpu.make_async_copy(near, onward, sem.at[0])] + pieces(inward, inner, rim, 3))
        run(here & plain & over, lambda: [pltpu.make_async_copy(near, onward, sem.at[0]), pltpu.make_async_copy(turned, inward, sem.at[3])])
        run(
            here & jnp.logical_not(plain) & over,
            lambda: pieces(onward, relay_inner, relay_rim, 0) + [pltpu.make_async_copy(turned, inward, sem.at[3])],
        )
    run(
        first_one,
        lambda: pieces(fwd_ref, relay_inner, relay_rim, 0)
        + [pltpu.make_async_copy(near, grad_ref, sem.at[3]), pltpu.make_async_copy(turned, mirror_ref, sem.at[4])],
    )


def call(body, z, args, outs, scratch, spaces, limit, flops=0, moved=0, out_space=pltpu.VMEM, aliases=None):
    return pl.pallas_call(
        functools.partial(body, z),
        out_shape=[jax.ShapeDtypeStruct(s, BF16) for s in outs],
        in_specs=[pl.BlockSpec(memory_space=s) for s in spaces],
        out_specs=[pl.BlockSpec(memory_space=out_space) for _ in outs],
        scratch_shapes=scratch,
        input_output_aliases=aliases or {},
        compiler_params=pltpu.CompilerParams(vmem_limit_bytes=limit),
        cost_estimate=pl.CostEstimate(flops=flops, bytes_accessed=moved, transcendentals=0),
    )(*args)


def chain_pairs(count):
    half = count // 2
    near, relay, crossed, turned = [(1, 0)], [], [], [(count - 1, 0)]
    for s in range(half):
        mirror = count - 1 - s
        if s % 2 == 0:
            near += [(s, s + 1), (mirror, mirror - 1)]
            if s > 0:
                crossed += [(s, s - 1), (mirror, mirror + 1)]
        else:
            if s + 1 < half:
                relay += [(mirror, s + 1), (s, mirror - 1)]
            turned += [(s, s - 1), (mirror, mirror + 1)]
    turned.remove((1, 0))
    return near, relay, crossed, turned


def tick(fwd_in, grad_in, saved_in, mirror_held, target, w_first, w_second):
    shape = fwd_in.shape[1:]
    rows, cols, chan = shape
    z = Sizes(rows, cols, chan)
    flat = lambda v: v.reshape(rows * cols, chan)
    fwd, grad, saved, held = (flat(v[0]) for v in (fwd_in, grad_in, saved_in, mirror_held))
    goal = flat(target)
    w1 = w_first[0].reshape(9, chan, chan)
    w2 = w_second[0].reshape(9, chan, chan)
    sections = lax.axis_size("section")
    any_, vm = pltpu.HBM, pltpu.VMEM
    six = (6 * cols, chan)

    to_up, to_down = call(
        halo_body, z, tuple(pltpu.with_memory_space_constraint(v, pltpu.HBM) for v in (fwd, grad, saved, held, goal)), (six, six),
        [pltpu.VMEM((5, 2, 4 * cols, chan), BF16), pltpu.SemaphoreType.DMA((5, 2))],
        [any_] * 5, 8 * MIB, 6_000_000_000, 0,
    )
    count = lax.axis_size("rows")
    above = lax.ppermute(to_down, "rows", [(i, i + 1) for i in range(count - 1)])
    below = lax.ppermute(to_up, "rows", [(i + 1, i) for i in range(count - 1)])

    x3 = pltpu.VMEM(((rows + 4) * cols, 3 * chan), BF16)
    acc = pltpu.VMEM(((rows + 2) * cols, chan), F32)
    wide = pltpu.VMEM(((rows + 4) * cols, chan), BF16)
    row_flops = 2 * cols * 9 * chan * chan
    two, size = 2 * cols, rows * cols
    main_shape, mid_shape = (size - 2 * two, chan), (size - two, chan)
    half = sections // 2
    mirror_pairs = [(s, sections - 1 - s) for s in range(sections)]
    near_pairs, relay_pairs, crossed_pairs, turned_pairs = chain_pairs(sections)
    y_inner, y_mid = call(
        inner_forward, z, (fwd, held, w1, w2), (main_shape, mid_shape),
        [x3, acc], [vm] * 4, 24 * MIB, 26 * row_flops, 12 * MIB,
    )
    to_decoder = lax.ppermute(y_inner, "section", mirror_pairs[:half])
    g_inner, g_mid = call(
        inner_backward, z, (grad, saved, held, w1, w2), (main_shape, mid_shape),
        [x3, acc, acc], [vm] * 5, 24 * MIB, 40 * row_flops, 12 * MIB,
    )
    to_encoder = lax.ppermute(g_inner, "section", mirror_pairs[half:-1])
    operands = (fwd, grad, saved, held, goal, above, below, w1, w2, y_inner, y_mid, g_inner, g_mid)
    results = ((size, chan), (2 * two, chan), (size, chan))
    scratch = [x3, acc, acc, wide, wide]
    first, rim, second = call(rest_body, z, operands, results, scratch, [vm] * 13, 24 * MIB, 70 * row_flops, 12 * MIB)
    mirror_rim = lax.ppermute(rim, "section", [p for p in mirror_pairs if p[1] != 0])
    turned = lax.ppermute(second, "section", crossed_pairs + turned_pairs)
    near = lax.ppermute(first, "section", near_pairs)
    (onward,) = call(pick_body, z, (to_decoder, to_encoder), (main_shape,), [], [vm] * 2, 8 * MIB, 0, MIB)
    relay_inner = lax.ppermute(onward, "section", relay_pairs)
    relay_rim = lax.ppermute(mirror_rim, "section", relay_pairs)
    (mirror_next,) = call(
        mirror_body, z, (to_decoder, to_encoder, mirror_rim), ((size, chan),),
        [pltpu.SemaphoreType.DMA((3,))], [vm] * 3, 8 * MIB, 0, MIB, pltpu.HBM,
    )
    fwd_next, grad_next, mirror_next = call(
        finish_body, z,
        (near, to_decoder, to_encoder, mirror_rim, relay_inner, relay_rim, turned, mirror_next),
        ((size, chan),) * 3, [pltpu.SemaphoreType.DMA((6,))], [vm] * 7 + [pltpu.HBM], 8 * MIB, 0, 2 * MIB, pltpu.HBM,
        aliases={7: 2},
    )
    full = lambda v: v.reshape((1,) + shape)
    return full(fwd_next), full(grad_next), full(mirror_next)


def solution(mesh):
    maps = P("section", "rows", None, None)
    weights = P("section", None, None, None, None)
    return jax.shard_map(
        tick,
        mesh=mesh,
        in_specs=(maps, maps, maps, maps, P("rows", None, None), weights, weights),
        out_specs=(maps, maps, maps),
        check_vma=False,
    )
```

```python
import functools

import jax
import jax.numpy as jnp
from jax import lax
from jax.experimental import pallas as pl
from jax.experimental.pallas import tpu as pltpu
from jax.sharding import PartitionSpec as P


BF16 = jnp.bfloat16
F32 = jnp.float32
NN = (((1,), (0,)), ((), ()))
NT = (((1,), (1,)), ((), ()))
MIB = 1 << 20


class Sizes:
    def __init__(self, rows, cols, chan):
        self.rows, self.cols, self.chan = rows, cols, chan


def roles():
    section = lax.axis_index("section")
    sections = lax.axis_size("section")
    row = lax.axis_index("rows")
    decoder = section >= sections // 2
    last = section == sections - 1
    top = row == 0
    bottom = row == lax.axis_size("rows") - 1
    return section, decoder, last, top, bottom


def silu(v):
    return v * jax.nn.sigmoid(v)


def silu_slope(pre):
    sig = jax.nn.sigmoid(pre)
    return sig * (1.0 + pre * (1.0 - sig))


def spread(z, x3, row, value):
    cols, chan = z.cols, z.chan
    count = value.shape[0] // cols
    wide = value.astype(F32).reshape(count, cols, chan)
    col = lax.broadcasted_iota(jnp.int32, wide.shape, 1)
    before = jnp.where(col == 0, 0.0, pltpu.roll(wide, 1, 1))
    after = jnp.where(col == cols - 1, 0.0, pltpu.roll(wide, cols - 1, 1))
    at = slice(row * cols, (row + count) * cols)
    x3[at, 0:chan] = before.reshape(count * cols, chan).astype(BF16)
    x3[at, chan : 2 * chan] = value.astype(BF16)
    x3[at, 2 * chan :] = after.reshape(count * cols, chan).astype(BF16)


def conv(z, x3, pieces, w, acc, flip):
    cols, chan = z.cols, z.chan
    size = sum(n for _, n in pieces) * cols

    def left(a, lanes):
        parts = []
        for start, n in pieces:
            first = (start + a) * cols
            if not isinstance(a, int):
                first = pl.multiple_of(first, cols)
            parts.append(x3[pl.ds(first, n * cols), lanes])
        return parts[0] if len(parts) == 1 else jnp.concatenate(parts, 0)

    def tap_row(a):
        if not flip:
            right = w[pl.ds(3 * a, 3)].reshape(3 * chan, chan)
            return lax.dot_general(left(a, slice(None)), right, NN, preferred_element_type=F32)
        total = None
        for b in range(3):
            right = w[3 * (2 - a) + 2 - b]
            part = lax.dot_general(left(a, slice(b * chan, (b + 1) * chan)), right, NT, preferred_element_type=F32)
            total = part if total is None else total + part
        return total

    for a in range(3):
        if a == 0:
            acc[0:size] = tap_row(0)
        else:
            acc[0:size] += tap_row(a)


def block_input(fwd, held, decoder):
    return fwd.astype(F32) + decoder.astype(F32) * held.astype(F32)


def block_grad(grad, held, decoder):
    return (grad.astype(F32) + (1.0 - decoder.astype(F32)) * held.astype(F32)).astype(BF16)


def halo_body(z, fwd, grad, saved, held, target, up_ref, down_ref, buf, sem):
    rows, cols = z.rows, z.cols
    _, decoder, last, _, _ = roles()
    edge = 4 * cols
    copies = []
    for i, ref in enumerate((fwd, grad, saved, held, target)):
        for e, start in enumerate((0, (rows - 4) * cols)):
            copies.append(pltpu.make_async_copy(ref.at[pl.ds(start, edge)], buf.at[i, e], sem.at[i, e]))
    for c in copies:
        c.start()
    for c in copies:
        c.wait()
    two = 2 * cols
    for e, ref in enumerate((up_ref, down_ref)):
        near = slice(0, two) if e == 0 else slice(two, edge)
        u = block_input(buf[0, e], buf[3, e], decoder).astype(BF16)
        g = block_grad(buf[1, e], buf[3, e], decoder)
        kept = buf[2, e]

        @pl.when(last)
        def _():
            ref[0:edge] = u
            ref[edge:] = buf[4, e][near]

        @pl.when(jnp.logical_not(last))
        def _():
            ref[0:two] = u[near]
            ref[two:edge] = kept[near]
            ref[edge:] = g[near]


def inner_forward(z, fwd, held, w1, w2, main_ref, mid_ref, x3, acc):
    rows, cols = z.rows, z.cols
    _, decoder, last, _, _ = roles()
    m1, m2 = (rows - 2) * cols, (rows - 4) * cols

    @pl.when(jnp.logical_or(jnp.logical_not(decoder), last))
    def _():
        u = block_input(fwd[...], held[...], decoder)
        spread(z, x3, 0, u.astype(BF16))
        conv(z, x3, [(0, rows - 2)], w1, acc, False)
        mid = silu(acc[0:m1]).astype(BF16)
        mid_ref[...] = mid
        spread(z, x3, 0, mid)
        conv(z, x3, [(0, rows - 4)], w2, acc, False)
        keep = slice(2 * cols, (rows - 2) * cols)
        main_ref[...] = (block_input(fwd[keep], held[keep], decoder) + acc[0:m2]).astype(BF16)


def inner_backward(z, grad, saved, held, w1, w2, main_ref, mid_ref, x3, acc, pre):
    rows, cols = z.rows, z.cols
    _, decoder, last, _, _ = roles()
    m1, m2 = (rows - 2) * cols, (rows - 4) * cols

    @pl.when(jnp.logical_and(decoder, jnp.logical_not(last)))
    def _():
        spread(z, x3, 0, saved[...])
        conv(z, x3, [(0, rows - 2)], w1, acc, False)
        pre[0:m1] = acc[0:m1]
        spread(z, x3, 0, block_grad(grad[...], held[...], decoder))
        conv(z, x3, [(0, rows - 2)], w2, acc, True)
        mid = (silu_slope(pre[0:m1]) * acc[0:m1]).astype(BF16)
        mid_ref[...] = mid
        spread(z, x3, 0, mid)
        conv(z, x3, [(0, rows - 4)], w1, acc, True)
        keep = slice(2 * cols, (rows - 2) * cols)
        g = block_grad(grad[keep], held[keep], decoder)
        main_ref[...] = (g.astype(F32) + acc[0:m2]).astype(BF16)


def zero_rows(z, value, lo, hi, top, bottom):
    cols = z.cols
    place = lax.broadcasted_iota(jnp.int32, value.shape, 0)
    outside = jnp.logical_or(
        jnp.logical_and(top, place < lo * cols),
        jnp.logical_and(bottom, place >= value.shape[0] - hi * cols),
    )
    return jnp.where(outside, jnp.zeros_like(value), value)


def whole_backward(z, kept, top_grad, w1, w2, x3, acc, pre, out_ref, top, bottom):
    rows, cols = z.rows, z.cols
    m1, m2 = (rows + 2) * cols, rows * cols
    spread(z, x3, 0, kept[...])
    conv(z, x3, [(0, rows + 2)], w1, acc, False)
    pre[0:m1] = acc[0:m1]
    spread(z, x3, 0, top_grad[...])
    conv(z, x3, [(0, rows + 2)], w2, acc, True)
    mid = (silu_slope(pre[0:m1]) * acc[0:m1]).astype(BF16)
    spread(z, x3, 0, zero_rows(z, mid, 1, 1, top, bottom))
    conv(z, x3, [(0, rows)], w1, acc, True)
    out_ref[...] = (top_grad[2 * cols : 2 * cols + m2].astype(F32) + acc[0:m2]).astype(BF16)


def encoder_rest(
    z, fwd, grad, saved, held, above, below, w1, w2, y_inner, y_mid, first_in, second_in,
    first_ref, second_ref, rim_ref, x3, acc, pre, kept, top_grad,
):
    rows, cols = z.rows, z.cols
    two, four, six = 2 * cols, 4 * cols, 6 * cols
    full = rows * cols
    section, decoder, _, top, bottom = roles()
    m1 = (rows - 2) * cols
    high = slice(full - two, full)

    @pl.when(jnp.logical_not(decoder))
    def _():
        first_ref[two : full - two] = y_inner[...]
        u = block_input(fwd[...], held[...], decoder).astype(BF16)
        spread(z, x3, 0, jnp.concatenate([above[0:two], u[0:two], u[full - two :], below[0:two]], 0))
        conv(z, x3, [(0, 2), (4, 2)], w1, acc, False)
        mid = zero_rows(z, silu(acc[0:four]).astype(BF16), 1, 1, top, bottom)
        spread(z, x3, 0, jnp.concatenate([mid[0:two], y_mid[0:two], y_mid[m1 - two :], mid[two:]], 0))
        conv(z, x3, [(0, 2), (4, 2)], w2, acc, False)
        first_ref[0:two] = (block_input(fwd[0:two], held[0:two], decoder) + acc[0:two]).astype(BF16)
        first_ref[high] = (block_input(fwd[high], held[high], decoder) + acc[two:four]).astype(BF16)
        kept[0:two] = above[two:four]
        kept[two : two + full] = saved[...]
        kept[two + full :] = below[two:four]
        top_grad[0:two] = above[four:six]
        top_grad[two : two + full] = block_grad(grad[...], held[...], decoder)
        top_grad[two + full :] = below[four:six]
        rim_ref[0:two] = first_ref[0:two]
        rim_ref[two:] = first_ref[full - two :]

    @pl.when(jnp.logical_not(decoder) & (section != 0))
    def _():
        whole_backward(z, kept, top_grad, w1, w2, x3, acc, pre, second_ref, top, bottom)

    @pl.when(section == 1)
    def _():
        first_ref[...] = second_ref[...]


def decoder_rest(
    z, fwd, grad, saved, held, target, above, below, w1, w2, y_inner, y_mid, g_inner, g_mid,
    first_ref, second_ref, rim_ref, x3, acc, pre, kept, top_grad,
):
    rows, cols = z.rows, z.cols
    two, four, six, eight = 2 * cols, 4 * cols, 6 * cols, 8 * cols
    full = rows * cols
    _, decoder, last, top, bottom = roles()
    m1 = (rows - 2) * cols
    high = slice(full - two, full)

    @pl.when(last)
    def _():
        u = block_input(fwd[...], held[...], decoder)
        ub = u.astype(BF16)
        spread(z, x3, 0, jnp.concatenate([above[0:four], ub[0:two], ub[full - two :], below[0:four]], 0))
        conv(z, x3, [(0, 4), (6, 4)], w1, acc, False)
        mid = zero_rows(z, silu(acc[0:eight]).astype(BF16), 3, 3, top, bottom)
        spread(z, x3, 0, jnp.concatenate([mid[0:four], y_mid[0:two], y_mid[m1 - two :], mid[four:]], 0))
        conv(z, x3, [(0, 4), (6, 4)], w2, acc, False)
        y_low = (jnp.concatenate([above[two:four].astype(F32), u[0:two]], 0) + acc[0:four]).astype(BF16)
        y_high = (jnp.concatenate([u[full - two :], below[0:two].astype(F32)], 0) + acc[four:eight]).astype(BF16)
        y = jnp.concatenate([y_low, y_inner[...], y_high], 0).astype(F32)
        goal = jnp.concatenate([above[four:six], target[...], below[four:six]], 0).astype(F32)
        top_grad[...] = zero_rows(z, (y - goal).astype(BF16), 2, 2, top, bottom)
        kept[0:two] = above[two:four]
        kept[two : two + full] = ub
        kept[two + full :] = below[0:two]
        whole_backward(z, kept, top_grad, w1, w2, x3, acc, pre, second_ref, top, bottom)
        first_ref[...] = second_ref[...]

    @pl.when(decoder & jnp.logical_not(last))
    def _():
        first_ref[two : full - two] = g_inner[...]
        spread(z, x3, 0, jnp.concatenate([above[two:four], saved[0:two], saved[high], below[two:four]], 0))
        conv(z, x3, [(0, 2), (4, 2)], w1, acc, False)
        pre[0:four] = acc[0:four]
        g_low = block_grad(grad[0:two], held[0:two], decoder)
        g_high = block_grad(grad[high], held[high], decoder)
        spread(z, x3, 0, jnp.concatenate([above[four:six], g_low, g_high, below[four:six]], 0))
        conv(z, x3, [(0, 2), (4, 2)], w2, acc, True)
        mid = (silu_slope(pre[0:four]) * acc[0:four]).astype(BF16)
        mid = zero_rows(z, mid, 1, 1, top, bottom)
        spread(z, x3, 0, jnp.concatenate([mid[0:two], g_mid[0:two], g_mid[m1 - two :], mid[two:]], 0))
        conv(z, x3, [(0, 2), (4, 2)], w1, acc, True)
        first_ref[0:two] = (g_low.astype(F32) + acc[0:two]).astype(BF16)
        first_ref[high] = (g_high.astype(F32) + acc[two:four]).astype(BF16)

        spread(z, x3, 0, above[0:two])
        spread(z, x3, 2, block_input(fwd[...], held[...], decoder).astype(BF16))
        spread(z, x3, 2 + rows, below[0:two])
        conv(z, x3, [(0, rows + 2)], w1, acc, False)
        hidden = silu(acc[0 : (rows + 2) * cols]).astype(BF16)
        spread(z, x3, 0, zero_rows(z, hidden, 1, 1, top, bottom))
        conv(z, x3, [(0, rows)], w2, acc, False)
        second_ref[...] = (block_input(fwd[...], held[...], decoder) + acc[0:full]).astype(BF16)

    @pl.when(decoder)
    def _():
        rim_ref[0:two] = first_ref[0:two]
        rim_ref[two:] = first_ref[full - two :]


def mirror_body(z, to_decoder, to_encoder, rim_to_decoder, rim_to_encoder, out_ref, sem):
    _, decoder, _, _, _ = roles()
    for here, inner, rim in (
        (decoder, to_decoder, rim_to_decoder),
        (jnp.logical_not(decoder), to_encoder, rim_to_encoder),
    ):

        @pl.when(here)
        def _():
            copies = pieces(z, out_ref, inner, rim, sem, 0)
            for c in copies:
                c.start()
            for c in copies:
                c.wait()


def pieces(z, ref, main, edges, sem, base):
    two, full = 2 * z.cols, z.rows * z.cols
    return [
        pltpu.make_async_copy(main, ref.at[pl.ds(two, full - 2 * two)], sem.at[base]),
        pltpu.make_async_copy(edges.at[pl.ds(0, two)], ref.at[pl.ds(0, two)], sem.at[base + 1]),
        pltpu.make_async_copy(edges.at[pl.ds(two, two)], ref.at[pl.ds(full - two, two)], sem.at[base + 2]),
    ]


def pick_body(z, to_decoder, to_encoder, out_ref):
    _, decoder, _, _, _ = roles()

    @pl.when(decoder)
    def _():
        out_ref[...] = to_decoder[...]

    @pl.when(jnp.logical_not(decoder))
    def _():
        out_ref[...] = to_encoder[...]


def finish_body(
    z, near, to_decoder, to_encoder, rim_to_decoder, rim_to_encoder, relay_inner, relay_rim, turned, mirror_in, fwd_ref, grad_ref, mirror_ref, sem
):
    section, decoder, _, _, _ = roles()
    half = lax.axis_size("section") // 2
    plain = section % 2 == 1 - decoder.astype(jnp.int32)
    joined = (section == half) | (section == half - 1)
    first_one = section == 0
    over = jnp.logical_not(joined | first_one)

    def run(here, copies):
        @pl.when(here)
        def _():
            made = copies()
            for c in made:
                c.start()
            for c in made:
                c.wait()

    for is_decoder in (False, True):
        onward, inward = (grad_ref, fwd_ref) if is_decoder else (fwd_ref, grad_ref)
        inner, rim = (to_decoder, rim_to_decoder) if is_decoder else (to_encoder, rim_to_encoder)
        here = decoder == is_decoder
        run(here & plain & joined, lambda: [pltpu.make_async_copy(near, onward, sem.at[0])] + pieces(z, inward, inner, rim, sem, 3))
        run(here & plain & over, lambda: [pltpu.make_async_copy(near, onward, sem.at[0]), pltpu.make_async_copy(turned, inward, sem.at[3])])
        run(
            here & jnp.logical_not(plain) & over,
            lambda: pieces(z, onward, relay_inner, relay_rim, sem, 0) + [pltpu.make_async_copy(turned, inward, sem.at[3])],
        )
    run(
        first_one,
        lambda: pieces(z, fwd_ref, relay_inner, relay_rim, sem, 0)
        + [pltpu.make_async_copy(near, grad_ref, sem.at[3]), pltpu.make_async_copy(turned, mirror_ref, sem.at[4])],
    )


def call(body, z, args, outs, scratch, spaces, limit, flops=0, moved=0, out_space=pltpu.VMEM, aliases=None):
    return pl.pallas_call(
        functools.partial(body, z),
        out_shape=[jax.ShapeDtypeStruct(s, BF16) for s in outs],
        in_specs=[pl.BlockSpec(memory_space=s) for s in spaces],
        out_specs=[pl.BlockSpec(memory_space=out_space) for _ in outs],
        scratch_shapes=scratch,
        input_output_aliases=aliases or {},
        compiler_params=pltpu.CompilerParams(vmem_limit_bytes=limit),
        cost_estimate=pl.CostEstimate(flops=flops, bytes_accessed=moved, transcendentals=0),
    )(*args)


def chain_pairs(count):
    half = count // 2
    near, relay, crossed, turned = [(1, 0)], [], [], [(count - 1, 0)]
    for s in range(half):
        mirror = count - 1 - s
        if s % 2 == 0:
            near += [(s, s + 1), (mirror, mirror - 1)]
            if s > 0:
                crossed += [(s, s - 1), (mirror, mirror + 1)]
        else:
            if s + 1 < half:
                relay += [(mirror, s + 1), (s, mirror - 1)]
            turned += [(s, s - 1), (mirror, mirror + 1)]
    turned.remove((1, 0))
    return near, relay, crossed, turned


def tick(fwd_in, grad_in, saved_in, mirror_held, target, w_first, w_second):
    shape = fwd_in.shape[1:]
    rows, cols, chan = shape
    z = Sizes(rows, cols, chan)
    flat = lambda v: v.reshape(rows * cols, chan)
    fwd, grad, saved, held = (flat(v[0]) for v in (fwd_in, grad_in, saved_in, mirror_held))
    goal = flat(target)
    w1 = w_first[0].reshape(9, chan, chan)
    w2 = w_second[0].reshape(9, chan, chan)
    sections = lax.axis_size("section")
    any_, vm = pltpu.HBM, pltpu.VMEM
    six = (6 * cols, chan)

    to_up, to_down = call(
        halo_body, z, tuple(pltpu.with_memory_space_constraint(v, pltpu.HBM) for v in (fwd, grad, saved, held, goal)), (six, six),
        [pltpu.VMEM((5, 2, 4 * cols, chan), BF16), pltpu.SemaphoreType.DMA((5, 2))],
        [any_] * 5, 8 * MIB, 6_000_000_000, 0,
    )
    count = lax.axis_size("rows")
    above = lax.ppermute(to_down, "rows", [(i, i + 1) for i in range(count - 1)])
    below = lax.ppermute(to_up, "rows", [(i + 1, i) for i in range(count - 1)])

    x3 = pltpu.VMEM(((rows + 4) * cols, 3 * chan), BF16)
    acc = pltpu.VMEM(((rows + 2) * cols, chan), F32)
    wide = pltpu.VMEM(((rows + 4) * cols, chan), BF16)
    row_flops = 2 * cols * 9 * chan * chan
    two, size = 2 * cols, rows * cols
    main_shape, mid_shape = (size - 2 * two, chan), (size - two, chan)
    half = sections // 2
    mirror_pairs = [(s, sections - 1 - s) for s in range(sections)]
    near_pairs, relay_pairs, crossed_pairs, turned_pairs = chain_pairs(sections)
    g_inner, g_mid = call(
        inner_backward, z, (grad, saved, held, w1, w2), (main_shape, mid_shape),
        [x3, acc, acc], [vm] * 5, 24 * MIB, 40 * row_flops, 12 * MIB,
    )
    to_encoder = lax.ppermute(g_inner, "section", mirror_pairs[half:-1])
    y_inner, y_mid = call(
        inner_forward, z, (fwd, held, w1, w2), (main_shape, mid_shape),
        [x3, acc], [vm] * 4, 24 * MIB, 26 * row_flops, 12 * MIB,
    )
    to_decoder = lax.ppermute(y_inner, "section", mirror_pairs[:half])
    main_args = (fwd, grad, saved, held)
    whole, rim_shape = (size, chan), (2 * two, chan)
    scratch = [x3, acc, acc, wide, wide]
    first, second, rim = call(
        decoder_rest, z, main_args + (goal, above, below, w1, w2, y_inner, y_mid, g_inner, g_mid),
        (whole, whole, rim_shape), scratch, [vm] * 13, 24 * MIB, 70 * row_flops, 12 * MIB,
    )
    rim_to_encoder = lax.ppermute(rim, "section", mirror_pairs[half:-1])
    first, second, rim = call(
        encoder_rest, z, main_args + (above, below, w1, w2, y_inner, y_mid, first, second),
        (whole, whole, rim_shape), scratch, [vm] * 12, 24 * MIB, 70 * row_flops, 12 * MIB, aliases={10: 0, 11: 1},
    )
    rim_to_decoder = lax.ppermute(rim, "section", mirror_pairs[:half])
    turned = lax.ppermute(second, "section", crossed_pairs + turned_pairs)
    near = lax.ppermute(first, "section", near_pairs)
    (onward,) = call(pick_body, z, (to_decoder, to_encoder), (main_shape,), [], [vm] * 2, 8 * MIB, 0, MIB)
    relay_inner = lax.ppermute(onward, "section", relay_pairs)
    (onward_rim,) = call(pick_body, z, (rim_to_decoder, rim_to_encoder), (rim_shape,), [], [vm] * 2, 8 * MIB, 0, MIB)
    relay_rim = lax.ppermute(onward_rim, "section", relay_pairs)
    arrived = (to_decoder, to_encoder, rim_to_decoder, rim_to_encoder)
    (mirror_next,) = call(
        mirror_body, z, arrived, (whole,),
        [pltpu.SemaphoreType.DMA((3,))], [vm] * 4, 8 * MIB, 0, MIB, pltpu.HBM,
    )
    fwd_next, grad_next, mirror_next = call(
        finish_body, z, (near,) + arrived + (relay_inner, relay_rim, turned, mirror_next),
        (whole,) * 3, [pltpu.SemaphoreType.DMA((6,))], [vm] * 8 + [pltpu.HBM], 8 * MIB, 0, 2 * MIB, pltpu.HBM,
        aliases={8: 2},
    )
    full = lambda v: v.reshape((1,) + shape)
    return full(fwd_next), full(grad_next), full(mirror_next)


def solution(mesh):
    maps = P("section", "rows", None, None)
    weights = P("section", None, None, None, None)
    return jax.shard_map(
        tick,
        mesh=mesh,
        in_specs=(maps, maps, maps, maps, P("rows", None, None), weights, weights),
        out_specs=(maps, maps, maps),
        check_vma=False,
    )
```
